32 devices in a mesh: fsdp: 4 (over z), context: 4 (over y, x), tensor: 2 (over core).
Axes of the slice: x: 2, y: 2, z: 4, core: 2. Of those that a mesh axis runs over, the one named last changes fastest.
Arguments:
- tokens: int32 [3, 4, 1024], P(None, 'fsdp'), may hold values from 0 to 49151
- lengths: int32 [3, 4], P(None, 'fsdp'), may hold values from 1024 to 1024, as said below
- loss_positions: int32 [3, 4, 128], P(None, 'fsdp'), may hold values from 0 to 1023
- teacher_ids: int32 [3, 4, 128, 64], P(None, 'fsdp'), may hold values from 0 to 49151
- label_ids: int32 [3, 4, 128], P(None, 'fsdp'), may hold values from 0 to 49151
- embedding: float32 [49152, 960], P(('context', 'tensor')), may hold values from -0.375 to 0.375
- incoming: float32 [1, 960, 1600], P(None, ('fsdp', 'tensor')), may hold values from -0.1875 to 0.1875
- outgoing: float32 [1, 960, 960], P(None, ('fsdp', 'tensor')), may hold values from -1.5 to 1.5
- expand: float32 [1, 960, 5120], P(None, ('fsdp', 'tensor')), may hold values from -0.1875 to 0.1875
- contract: float32 [1, 2560, 960], P(None, ('fsdp', 'tensor')), may hold values from -0.125 to 0.125
- scales: float32 [3, 960], P(None, ('fsdp', 'tensor')), may hold values from 0.5 to 1.5
- drift_embedding: float32 [49152, 960], P(('context', 'tensor')), may hold values from -9.536743e-07 to 9.536743e-07
- incoming_first_moment: float32 [1, 960, 1600], P(None, ('fsdp', 'tensor')), may hold values from -9.536743e-07 to 9.536743e-07
- drift_outgoing: float32 [1, 960, 960], P(None, ('fsdp', 'tensor')), may hold values from -9.536743e-07 to 9.536743e-07
- drift_expand: float32 [1, 960, 5120], P(None, ('fsdp', 'tensor')), may hold values from -9.536743e-07 to 9.536743e-07
- drift_contract: float32 [1, 2560, 960], P(None, ('fsdp', 'tensor')), may hold values from -9.536743e-07 to 9.536743e-07
- drift_scales: float32 [3, 960], P(None, ('fsdp', 'tensor')), may hold values from -9.536743e-07 to 9.536743e-07
- power_embedding: float32 [49152, 960], P(('context', 'tensor')), may hold values from 9.2249626e-14 to 3.68297e-13
- incoming_second_moment: float32 [1, 960, 1600], P(None, ('fsdp', 'tensor')), may hold values from 9.2249626e-14 to 3.68297e-13
- power_outgoing: float32 [1, 960, 960], P(None, ('fsdp', 'tensor')), may hold values from 9.2249626e-14 to 3.68297e-13
- power_expand: float32 [1, 960, 5120], P(None, ('fsdp', 'tensor')), may hold values from 9.2249626e-14 to 3.68297e-13
- power_contract: float32 [1, 2560, 960], P(None, ('fsdp', 'tensor')), may hold values from 9.2249626e-14 to 3.68297e-13
- power_scales: float32 [3, 960], P(None, ('fsdp', 'tensor')), may hold values from 9.2249626e-14 to 3.68297e-13
Outputs:
- loss_value: float32 [], replicated
- grad_norm: float32 [], replicated
- next_embedding: float32 [49152, 960], P(('context', 'tensor'))
- next_incoming: float32 [1, 960, 1600], P(None, ('fsdp', 'tensor'))
- next_outgoing: float32 [1, 960, 960], P(None, ('fsdp', 'tensor'))
- next_expand: float32 [1, 960, 5120], P(None, ('fsdp', 'tensor'))
- next_contract: float32 [1, 2560, 960], P(None, ('fsdp', 'tensor'))
- next_scales: float32 [3, 960], P(None, ('fsdp', 'tensor'))
- moment_embedding: float32 [49152, 960], P(('context', 'tensor'))
- moment_incoming: float32 [1, 960, 1600], P(None, ('fsdp', 'tensor'))
- moment_outgoing: float32 [1, 960, 960], P(None, ('fsdp', 'tensor'))
- moment_expand: float32 [1, 960, 5120], P(None, ('fsdp', 'tensor'))
- moment_contract: float32 [1, 2560, 960], P(None, ('fsdp', 'tensor'))
- moment_scales: float32 [3, 960], P(None, ('fsdp', 'tensor'))
- square_embedding: float32 [49152, 960], P(('context', 'tensor'))
- square_incoming: float32 [1, 960, 1600], P(None, ('fsdp', 'tensor'))
- square_outgoing: float32 [1, 960, 960], P(None, ('fsdp', 'tensor'))
- square_expand: float32 [1, 960, 5120], P(None, ('fsdp', 'tensor'))
- square_contract: float32 [1, 2560, 960], P(None, ('fsdp', 'tensor'))
- square_scales: float32 [3, 960], P(None, ('fsdp', 'tensor'))
The draws below stay inside these ranges and needn't reach their ends.
Inputs may be any that keep to these rules, and one draw needn't show every extreme that they name: `lengths`: in each of the 3 micro-batches one sequence has exactly 1024 tokens. `loss_positions`: a loss position is this value modulo the sequence's length.
All inputs are finite; a program needn't handle non-finite values.
Results may differ from the reference program's by a relative error of at most 0.0065.
The reference program's roundings to bfloat16 on the way count: a program that leaves them out, or rounds other values in their place, can miss the bound.
Values may be sent and summed in bfloat16 or wider, within the bound.
A program may use at most 512 MiB of HBM per device.

```python
import math
import jax
import jax.numpy as jnp
import numpy as np
from jax import lax

MODEL_WIDTH = 960
QUERY_HEADS = 15
KEY_VALUE_HEADS = 5
HEAD_SIZE = 64
FF = 2560
V = 49152
LAYER_COUNT = 1
MB = 3
MIN_LEN = 1024
P_SIZE = 128
TEACH = 64
STEP = 10
SEQUENCE_SLOTS = 1024
SEQS_MB = 4
NPOS = 1536
PARAMETER_COUNT = 57019200


def draw_lengths(key, part):
    first_key, second_key = jax.random.split(jax.random.fold_in(key, 11))
    drawn = jax.random.randint(first_key, (MB, SEQS_MB), MIN_LEN, SEQUENCE_SLOTS + 1)
    picked = jax.random.randint(second_key, (MB, 1), 0, SEQS_MB)
    column = jnp.arange(SEQS_MB)[None, :]
    return jnp.where(column == picked, SEQUENCE_SLOTS, drawn).astype(jnp.int32)


def place_ends(values, own_key, low, high):
    longest = values.shape.index(max(values.shape))
    spots = []
    for shift in (0, 1):
        where = [jax.random.randint(jax.random.fold_in(own_key, axis), (), 0, length) for axis, length in enumerate(values.shape)]
        where[longest] = (where[longest] + shift) % values.shape[longest]
        spots.append(tuple(where))
    return values.at[spots[0]].set(low).at[spots[1]].set(high)


def block_scale(own_key, dims, shards, smallest, top_value):
    def one(dim, blocks):
        heights = jax.random.uniform(jax.random.fold_in(jax.random.fold_in(own_key, 6), dim), (blocks,), jnp.float32, smallest / len(shards), top_value / len(shards))
        return jnp.repeat(jnp.exp(heights), dims[dim] // blocks).reshape((-1,) + (1,) * (len(dims) - dim - 1))

    level = one(*shards[0])
    for cut in shards[1:]:
        level = level * one(*cut)
    return level


def rank_bounds(count, skew):
    portions = [(1 << 20) // math.isqrt(rank ** skew) + 1 for rank in range(1, count + 1)]
    spread = 1 + sum(portions) // (1 << 30)
    return np.cumsum(np.array([max(1, weight // spread) for weight in portions]))


def ranked_ids(own_key, extent, number_of, lean):
    listing = rank_bounds(number_of, lean)
    ticket = jax.random.randint(jax.random.fold_in(own_key, 1), extent, 0, int(listing[number_of - 1]))
    standing = jnp.searchsorted(jnp.asarray(listing, jnp.int32), ticket, side="right")
    return jax.random.permutation(jax.random.fold_in(own_key, 2), number_of)[standing].astype(jnp.int32)


def gaussian(own_key, shape, deviation, bound, cuts=(), kind=jnp.bfloat16):
    array = jax.random.normal(own_key, shape, jnp.float32) * deviation
    if len(cuts) > 0:
        array = block_scale(own_key, shape, cuts, -0.22, 0.18) * array
    return jnp.clip(array, min=-bound, max=bound).astype(kind)


def setup_inputs(seed: int = 0) -> dict:
    arg_keys = jax.random.split(jax.random.key(seed), 24)
    return {
        "tokens": place_ends(ranked_ids(arg_keys[0], (MB, SEQS_MB, SEQUENCE_SLOTS), V, 2), jax.random.fold_in(arg_keys[0], 3), 0, V - 1).astype(jnp.int32),
        "lengths": draw_lengths(jax.random.fold_in(arg_keys[23], 71), 0),
        "loss_positions": place_ends(jax.random.randint(arg_keys[2], (MB, SEQS_MB, P_SIZE), 0, SEQUENCE_SLOTS), jax.random.fold_in(arg_keys[2], 1), 0, SEQUENCE_SLOTS - 1).astype(jnp.int32),
        "teacher_ids": place_ends(ranked_ids(arg_keys[3], (MB, SEQS_MB, P_SIZE, TEACH), V, 2), jax.random.fold_in(arg_keys[3], 3), 0, V - 1).astype(jnp.int32),
        "label_ids": place_ends(jax.random.randint(arg_keys[4], (MB, SEQS_MB, P_SIZE), 0, V), jax.random.fold_in(arg_keys[4], 1), 0, V - 1).astype(jnp.int32),
        "embedding": gaussian(arg_keys[5], (V, MODEL_WIDTH), (MODEL_WIDTH // 4) ** -0.5, 0.375, ((0, 8),), jnp.float32),
        "incoming": gaussian(arg_keys[6], (LAYER_COUNT, MODEL_WIDTH, (QUERY_HEADS + 2 * KEY_VALUE_HEADS) * HEAD_SIZE), MODEL_WIDTH ** -0.5, 0.1875, ((1, 8),), jnp.float32),
        "outgoing": gaussian(arg_keys[7], (LAYER_COUNT, QUERY_HEADS * HEAD_SIZE, MODEL_WIDTH), (QUERY_HEADS * HEAD_SIZE // 64) ** -0.5, 1.5, ((1, 8),), jnp.float32),
        "expand": gaussian(arg_keys[8], (LAYER_COUNT, MODEL_WIDTH, 2 * FF), MODEL_WIDTH ** -0.5, 0.1875, ((1, 8),), jnp.float32),
        "contract": gaussian(arg_keys[9], (LAYER_COUNT, FF, MODEL_WIDTH), FF ** -0.5, 0.125, ((1, 8),), jnp.float32),
        "scales": jnp.clip(1.0 + 0.1 * jax.random.normal(arg_keys[10], (2 * LAYER_COUNT + 1, MODEL_WIDTH), jnp.float32), 0.5, 1.5),
        "drift_embedding": gaussian(arg_keys[11], (V, MODEL_WIDTH), (0.00111 * PARAMETER_COUNT ** -0.5), 9.5367431640625e-07, ((0, 8),), jnp.float32),
        "incoming_first_moment": gaussian(arg_keys[12], (LAYER_COUNT, MODEL_WIDTH, (QUERY_HEADS + 2 * KEY_VALUE_HEADS) * HEAD_SIZE), (0.00111 * PARAMETER_COUNT ** -0.5), 9.5367431640625e-07, ((1, 8),), jnp.float32),
        "drift_outgoing": gaussian(arg_keys[13], (LAYER_COUNT, QUERY_HEADS * HEAD_SIZE, MODEL_WIDTH), (0.00111 * PARAMETER_COUNT ** -0.5), 9.5367431640625e-07, ((1, 8),), jnp.float32),
        "drift_expand": gaussian(arg_keys[14], (LAYER_COUNT, MODEL_WIDTH, 2 * FF), (0.00111 * PARAMETER_COUNT ** -0.5), 9.5367431640625e-07, ((1, 8),), jnp.float32),
        "drift_contract": gaussian(arg_keys[15], (LAYER_COUNT, FF, MODEL_WIDTH), (0.00111 * PARAMETER_COUNT ** -0.5), 9.5367431640625e-07, ((1, 8),), jnp.float32),
        "drift_scales": gaussian(arg_keys[16], (2 * LAYER_COUNT + 1, MODEL_WIDTH), (0.00111 * PARAMETER_COUNT ** -0.5), 9.5367431640625e-07, ((1, 8),), jnp.float32),
        "power_embedding": jnp.clip(jnp.exp(math.log(3.6829699988534526e-13) - 1.3843914 * jax.random.uniform(arg_keys[17], (V, MODEL_WIDTH), jnp.float32) ** block_scale(arg_keys[17], (V, MODEL_WIDTH), ((0, 8),), -0.2, 0.2)), 9.224962644899942e-14, 3.6829699988534526e-13),
        "incoming_second_moment": jnp.clip(jnp.exp(math.log(3.6829699988534526e-13) - 1.3843914 * jax.random.uniform(arg_keys[18], (LAYER_COUNT, MODEL_WIDTH, (QUERY_HEADS + 2 * KEY_VALUE_HEADS) * HEAD_SIZE), jnp.float32) ** block_scale(arg_keys[18], (LAYER_COUNT, MODEL_WIDTH, (QUERY_HEADS + 2 * KEY_VALUE_HEADS) * HEAD_SIZE), ((1, 8),), -0.2, 0.2)), 9.224962644899942e-14, 3.6829699988534526e-13),
        "power_outgoing": jnp.clip(jnp.exp(math.log(3.6829699988534526e-13) - 1.3843914 * jax.random.uniform(arg_keys[19], (LAYER_COUNT, QUERY_HEADS * HEAD_SIZE, MODEL_WIDTH), jnp.float32) ** block_scale(arg_keys[19], (LAYER_COUNT, QUERY_HEADS * HEAD_SIZE, MODEL_WIDTH), ((1, 8),), -0.2, 0.2)), 9.224962644899942e-14, 3.6829699988534526e-13),
        "power_expand": jnp.clip(jnp.exp(math.log(3.6829699988534526e-13) - 1.3843914 * jax.random.uniform(arg_keys[20], (LAYER_COUNT, MODEL_WIDTH, 2 * FF), jnp.float32) ** block_scale(arg_keys[20], (LAYER_COUNT, MODEL_WIDTH, 2 * FF), ((1, 8),), -0.2, 0.2)), 9.224962644899942e-14, 3.6829699988534526e-13),
        "power_contract": jnp.clip(jnp.exp(math.log(3.6829699988534526e-13) - 1.3843914 * jax.random.uniform(arg_keys[21], (LAYER_COUNT, FF, MODEL_WIDTH), jnp.float32) ** block_scale(arg_keys[21], (LAYER_COUNT, FF, MODEL_WIDTH), ((1, 8),), -0.2, 0.2)), 9.224962644899942e-14, 3.6829699988534526e-13),
        "power_scales": jnp.clip(jnp.exp(math.log(3.6829699988534526e-13) - 1.3843914 * jax.random.uniform(arg_keys[22], (2 * LAYER_COUNT + 1, MODEL_WIDTH), jnp.float32) ** block_scale(arg_keys[22], (2 * LAYER_COUNT + 1, MODEL_WIDTH), ((1, 8),), -0.2, 0.2)), 9.224962644899942e-14, 3.6829699988534526e-13),
    }


EPSILON = 1e-05
THETA = 100000.0
CLIP = 0.01
BETA_ONE = 0.9
BETA_TWO = 0.95
ADAM_EPSILON = 1e-08
DECAY = 0.1
RATE_MATRIX = 0.05
RATE_GAIN = 0.5
MASKED = -1e+30
HIGH = lax.Precision.HIGHEST

@jax.custom_vjp
def reduced_copy(v):
    return lax.optimization_barrier(v.astype(jnp.bfloat16)).astype(jnp.float32)

@jax.custom_vjp
def low_back(v):
    return v

def low_keep(v):
    return (reduced_copy(v), None)

def low_pass(kept, grad):
    return (grad,)

def back_keep(v):
    return (v, None)

def back_low(kept, grad):
    return (reduced_copy(grad),)
reduced_copy.defvjp(low_keep, low_pass)
low_back.defvjp(back_keep, back_low)

def product(left, right):
    return jnp.dot(left, right, precision=HIGH)

def rmsnorm(value_rows, gain):
    return value_rows * lax.rsqrt(lax.optimization_barrier(jnp.mean(value_rows * value_rows, axis=-1, keepdims=True)) + EPSILON) * gain

def rotary_apply(value_rows, loss_places):
    half = value_rows.shape[-1] // 2
    freqs = THETA ** (-jnp.arange(half, dtype=jnp.float32) * 2.0 / value_rows.shape[-1])
    angles = loss_places.astype(jnp.float32)[:, None] * freqs[None, :]
    cosine = jnp.cos(angles)[:, None, :]
    sine = jnp.sin(angles)[:, None, :]
    first, second = (value_rows[..., :half], value_rows[..., half:])
    return jnp.concatenate([first * cosine - second * sine, first * sine + second * cosine], axis=-1)

def attend(query_rows, key_collection, value_collection, length):
    query_group = QUERY_HEADS // KEY_VALUE_HEADS
    row_extent = min(512, SEQUENCE_SLOTS)
    keyplace = jnp.arange(SEQUENCE_SLOTS).astype(jnp.int32)

    def one_block(position_offset):
        weight_slab = lax.dynamic_slice_in_dim(query_rows, position_offset, row_extent, 0).reshape(row_extent, KEY_VALUE_HEADS, query_group, HEAD_SIZE)
        scores = low_back(jnp.einsum('bhgd,khd->hgbk', weight_slab, key_collection, precision=HIGH) * HEAD_SIZE ** (-0.5))
        rowplace = position_offset + jnp.arange(row_extent).astype(jnp.int32)
        allowed = (keyplace[None, :] <= rowplace[:, None]) & (keyplace[None, :] < length)
        scores = jnp.where(allowed[None, None], scores, MASKED)
        chances = low_back(reduced_copy(jax.nn.softmax(scores, axis=-1)))
        mixed = jnp.einsum('hgbk,khd->bhgd', chances, value_collection, precision=HIGH)
        return mixed.reshape(row_extent, QUERY_HEADS * HEAD_SIZE)
    offsets = (jnp.arange(SEQUENCE_SLOTS // row_extent) * row_extent).astype(jnp.int32)
    return lax.map(jax.checkpoint(one_block), offsets).reshape(SEQUENCE_SLOTS, QUERY_HEADS * HEAD_SIZE)

def layer_forward(residual, incoming, outgoing, expand, contract, gain_attn, gain_ffn, loss_places, length):
    query_width = QUERY_HEADS * HEAD_SIZE
    key_width = KEY_VALUE_HEADS * HEAD_SIZE
    normed = low_back(reduced_copy(rmsnorm(residual, reduced_copy(gain_attn))))
    joined_heads = low_back(product(normed, reduced_copy(incoming)))
    query_rows = reduced_copy(rotary_apply(joined_heads[:, :query_width].reshape(SEQUENCE_SLOTS, QUERY_HEADS, HEAD_SIZE), loss_places))
    key_collection = reduced_copy(rotary_apply(joined_heads[:, query_width:query_width + key_width].reshape(SEQUENCE_SLOTS, KEY_VALUE_HEADS, HEAD_SIZE), loss_places))
    value_collection = reduced_copy(joined_heads[:, query_width + key_width:].reshape(SEQUENCE_SLOTS, KEY_VALUE_HEADS, HEAD_SIZE))
    attended = low_back(reduced_copy(attend(query_rows, key_collection, value_collection, length)))
    middle = residual + low_back(product(attended, reduced_copy(outgoing)))
    normed_ffn = low_back(reduced_copy(rmsnorm(middle, reduced_copy(gain_ffn))))
    gate_up = low_back(product(normed_ffn, reduced_copy(expand)))
    hidden = low_back(reduced_copy(jax.nn.silu(gate_up[:, :FF]) * gate_up[:, FF:]))
    return middle + low_back(product(hidden, reduced_copy(contract)))

def sequence_loss(weights, token_row, length, raw_places, teacher_row, label_row):
    embedding, incoming, outgoing, expand, contract, scales = weights
    table = reduced_copy(embedding)
    residual = low_back(jnp.take(table, token_row, axis=0))
    loss_places = jnp.arange(SEQUENCE_SLOTS).astype(jnp.int32)
    for number in range(LAYER_COUNT):
        residual = layer_forward(residual, incoming[number], outgoing[number], expand[number], contract[number], scales[2 * number], scales[2 * number + 1], loss_places, length)
    final = low_back(reduced_copy(rmsnorm(residual, reduced_copy(scales[2 * LAYER_COUNT]))))
    chosen = jnp.take(final, raw_places % length, axis=0)
    logits = low_back(jnp.dot(chosen, table.T, precision=HIGH))
    log_total = jax.nn.logsumexp(logits, axis=-1)
    teacher_part = lax.optimization_barrier(jnp.mean(jnp.take_along_axis(logits, teacher_row, axis=1), axis=1))
    label_part = jnp.take_along_axis(logits, label_row[:, None], axis=1)[:, 0]
    counts = lax.optimization_barrier(jnp.sum((teacher_row[:, :, None] == teacher_row[:, None, :]).astype(jnp.float32), axis=-1))
    entropy_part = lax.optimization_barrier(jnp.mean(jnp.log(counts / TEACH), axis=1))
    return jnp.sum(entropy_part + 2.0 * log_total - teacher_part - label_part)

def adamw(weight, grad, drift, power, rate, decay):
    moment = BETA_ONE * drift + (1.0 - BETA_ONE) * grad
    square = BETA_TWO * power + (1.0 - BETA_TWO) * grad * grad
    mean_hat = moment / (1.0 - BETA_ONE ** STEP)
    square_hat = square / (1.0 - BETA_TWO ** STEP)
    fresh = weight - rate * (mean_hat / (jnp.sqrt(square_hat) + ADAM_EPSILON) + decay * weight)
    return (fresh, moment, square)

def reference(tokens, lengths, loss_positions, teacher_ids, label_ids, embedding, incoming, outgoing, expand, contract, scales, drift_embedding, incoming_first_moment, drift_outgoing, drift_expand, drift_contract, drift_scales, power_embedding, incoming_second_moment, power_outgoing, power_expand, power_contract, power_scales):
    weights = (embedding, incoming, outgoing, expand, contract, scales)
    total_seqs = tokens.shape[0] * tokens.shape[1]
    items = (tokens.reshape(total_seqs, SEQUENCE_SLOTS), lengths.reshape(total_seqs), loss_positions.reshape(total_seqs, P_SIZE), teacher_ids.reshape(total_seqs, P_SIZE, TEACH), label_ids.reshape(total_seqs, P_SIZE))
    checked = jax.checkpoint(sequence_loss)

    def objective(params):

        def accumulate(carry, item):
            return (carry + checked(params, *item), None)
        summed, _ = lax.scan(accumulate, jnp.zeros((), jnp.float32), items)
        return summed / NPOS
    loss_value, pullback = jax.vjp(objective, weights)
    grads = pullback(jnp.ones((), jnp.float32))[0]
    grad_norm = jnp.sqrt(sum((jnp.sum(grad * grad) for grad in grads)))
    factor = CLIP / jnp.maximum(grad_norm, CLIP)
    drifts = (drift_embedding, incoming_first_moment, drift_outgoing, drift_expand, drift_contract, drift_scales)
    powers = (power_embedding, incoming_second_moment, power_outgoing, power_expand, power_contract, power_scales)
    rates = (RATE_MATRIX, RATE_MATRIX, RATE_MATRIX, RATE_MATRIX, RATE_MATRIX, RATE_GAIN)
    decays = (DECAY, DECAY, DECAY, DECAY, DECAY, 0.0)
    updated = [adamw(weights[index], grads[index] * factor, drifts[index], powers[index], rates[index], decays[index]) for index in range(6)]
    return (loss_value, grad_norm, updated[0][0], updated[1][0], updated[2][0], updated[3][0], updated[4][0], updated[5][0], updated[0][1], updated[1][1], updated[2][1], updated[3][1], updated[4][1], updated[5][1], updated[0][2], updated[1][2], updated[2][2], updated[3][2], updated[4][2], updated[5][2])
```

```python
import functools

import jax
import jax.numpy as jnp
from jax import lax
from jax.experimental import pallas as pl
from jax.experimental.pallas import tpu as pltpu
from jax.sharding import PartitionSpec as P

QUERY_HEADS = 15
KEY_VALUE_HEADS = 5
GROUP = QUERY_HEADS // KEY_VALUE_HEADS
HEAD_SIZE = 64
FF = 2560
LAYER_COUNT = 1
TEACH = 64
STEP = 10


EPSILON = 1e-05
THETA = 100000.0
CLIP = 0.01
BETA_ONE = 0.9
BETA_TWO = 0.95
ADAM_EPSILON = 1e-08
DECAY = 0.1
RATE_MATRIX = 0.05
RATE_GAIN = 0.5
MASKED = -1e30
PLANE = ("context", "tensor")
SHARDS = ("fsdp", "tensor")
EVERYONE = ("fsdp", "context", "tensor")
LANES = 128
SUBLANES = 8


def matmul(left, right):
    return jnp.dot(left, right, preferred_element_type=jnp.float32)


def across(left, right):
    return lax.dot_general(
        left, right, (((0,), (0,)), ((), ())), preferred_element_type=jnp.float32
    )


def against(left, right):
    return lax.dot_general(
        left, right, (((1,), (1,)), ((), ())), preferred_element_type=jnp.float32
    )


def rounded(value_rows):
    return lax.optimization_barrier(value_rows.astype(jnp.bfloat16)).astype(jnp.float32)


def rmsnorm(value_rows, gain):
    return (
        value_rows
        * lax.rsqrt(jnp.mean(value_rows * value_rows, axis=-1, keepdims=True) + EPSILON)
        * gain
    )


def rotary_tables(places):
    half = HEAD_SIZE // 2
    freqs = THETA ** (-jnp.arange(half, dtype=jnp.float32) * 2.0 / HEAD_SIZE)
    angles = places.astype(jnp.float32)[:, None] * freqs[None, :]
    return jnp.cos(angles), jnp.sin(angles)


def rotate(heads, cosine, sine):
    half = HEAD_SIZE // 2
    first, second = heads[..., :half], heads[..., half:]
    return jnp.concatenate(
        [first * cosine - second * sine, first * sine + second * cosine], axis=-1
    )


def adamw(weight, grad, drift, power, rate, decay):
    moment = BETA_ONE * drift + (1.0 - BETA_ONE) * grad
    square = BETA_TWO * power + (1.0 - BETA_TWO) * grad * grad
    mean_hat = moment / (1.0 - BETA_ONE**STEP)
    square_hat = square / (1.0 - BETA_TWO**STEP)
    fresh = weight - rate * (mean_hat / (jnp.sqrt(square_hat) + ADAM_EPSILON) + decay * weight)
    return (fresh, moment, square)


def masked_scores(query, key, first_row, length):
    scores = against(query, key) * HEAD_SIZE ** (-0.5)
    count = query.shape[0] // GROUP
    row = lax.broadcasted_iota(jnp.int32, (count, key.shape[0]), 0) + first_row
    column = lax.broadcasted_iota(jnp.int32, (count, key.shape[0]), 1)
    allowed = (column <= row) & (column < length)
    allowed = jnp.concatenate([allowed] * GROUP, axis=0)
    return jnp.where(allowed, scores, MASKED)


def forward_kernel(bounds, q_ref, k_ref, v_ref, out_ref, total_ref):
    b = pl.program_id(0)
    scores = masked_scores(q_ref[...], k_ref[...], bounds[0], bounds[1 + b])
    top = jnp.max(scores, axis=-1, keepdims=True)
    powers = jnp.exp(scores - top)
    total = jnp.sum(powers, axis=-1, keepdims=True)
    chances = (powers * (1.0 / total)).astype(jnp.bfloat16)
    out_ref[...] = matmul(chances, v_ref[...]).astype(jnp.bfloat16)
    total_ref[...] = top + jnp.log(total)


def backward_kernel(bounds, q_ref, k_ref, v_ref, g_ref, total_ref, dq_ref, dk_ref, dv_ref):
    b = pl.program_id(0)
    query, key, value, grad = q_ref[...], k_ref[...], v_ref[...], g_ref[...]
    scores = masked_scores(query, key, bounds[0], bounds[1 + b])
    chances = jnp.exp(scores - total_ref[...])
    dv_ref[...] = across(chances.astype(jnp.bfloat16), grad)
    grad_chances = against(grad, value).astype(jnp.bfloat16).astype(jnp.float32)
    mean = jnp.sum(chances * grad_chances, axis=-1, keepdims=True)
    grad_scores = (chances * (grad_chances - mean)).astype(jnp.bfloat16)
    dq_ref[...] = matmul(grad_scores, key) * HEAD_SIZE ** (-0.5)
    dk_ref[...] = across(grad_scores, query) * HEAD_SIZE ** (-0.5)


def head_block(rows, width):
    return pl.BlockSpec((None, None, rows, width), lambda b, g, bounds: (b, g, 0, 0))


def attention_forward(bounds, query, key, value):
    batches, heads, rows, size = query.shape
    slots = key.shape[2]
    cost = pl.CostEstimate(
        flops=4 * batches * heads * rows * slots * size,
        bytes_accessed=2 * batches * heads * (2 * rows + 2 * slots) * size,
        transcendentals=batches * heads * rows * slots,
    )
    return pl.pallas_call(
        forward_kernel,
        name="attention_forward",
        grid_spec=pltpu.PrefetchScalarGridSpec(
            num_scalar_prefetch=1,
            grid=(batches, heads),
            in_specs=[head_block(rows, size), head_block(slots, size), head_block(slots, size)],
            out_specs=[head_block(rows, size), head_block(rows, 1)],
        ),
        out_shape=[
            jax.ShapeDtypeStruct(query.shape, jnp.bfloat16),
            jax.ShapeDtypeStruct((batches, heads, rows, 1), jnp.float32),
        ],
        cost_estimate=cost,
    )(bounds, query, key, value)


def attention_backward(bounds, query, key, value, grad, total):
    batches, heads, rows, size = query.shape
    slots = key.shape[2]
    cost = pl.CostEstimate(
        flops=10 * batches * heads * rows * slots * size,
        bytes_accessed=2 * batches * heads * (4 * rows + 6 * slots) * size,
        transcendentals=batches * heads * rows * slots,
    )
    return pl.pallas_call(
        backward_kernel,
        name="attention_backward",
        grid_spec=pltpu.PrefetchScalarGridSpec(
            num_scalar_prefetch=1,
            grid=(batches, heads),
            in_specs=[
                head_block(rows, size),
                head_block(slots, size),
                head_block(slots, size),
                head_block(rows, size),
                head_block(rows, 1),
            ],
            out_specs=[head_block(rows, size), head_block(slots, size), head_block(slots, size)],
        ),
        out_shape=[
            jax.ShapeDtypeStruct(query.shape, jnp.float32),
            jax.ShapeDtypeStruct(key.shape, jnp.float32),
            jax.ShapeDtypeStruct(key.shape, jnp.float32),
        ],
        cost_estimate=cost,
    )(bounds, query, key, value, grad, total)


def frequency_kernel(per_step, high_ref, low_ref, share_ref, out_ref):
    tiles = out_ref.shape[1] // LANES
    entries = high_ref.shape[-1]
    row = lax.broadcasted_iota(jnp.int32, (tiles * SUBLANES, entries), 0)
    lane = lax.broadcasted_iota(jnp.int32, (LANES, entries), 0)

    def one_group(group, carry):
        high = high_ref[pl.ds(group, 1), :]
        low = low_ref[pl.ds(group, 1), :]
        share = share_ref[...]
        left = jnp.where(row == high, share, 0.0).astype(jnp.bfloat16)
        right = jnp.where(lane == low, 1.0, 0.0).astype(jnp.bfloat16)
        counts = against(left, right)
        start = pl.multiple_of(group * SUBLANES, SUBLANES)
        for tile in range(tiles):
            out_ref[pl.ds(start, SUBLANES), tile * LANES : (tile + 1) * LANES] = counts[
                tile * SUBLANES : (tile + 1) * SUBLANES
            ]
        return carry

    lax.fori_loop(0, per_step, one_group, 0)


def frequencies_of(teacher, labels, start, vocab_rows):
    positions = teacher.shape[0]
    groups = positions // SUBLANES
    ids = jnp.concatenate([teacher, labels[:, None]], axis=1) - start
    inside = (ids >= 0) & (ids < vocab_rows)
    spot = (jnp.arange(positions, dtype=jnp.int32) % SUBLANES)[:, None]
    high = jnp.where(inside, (ids // LANES) * SUBLANES + spot, -1)
    low = jnp.where(inside, ids % LANES, -1)
    pad = -(SUBLANES * (TEACH + 1)) % LANES

    def packed(value):
        value = value.reshape(groups, SUBLANES * (TEACH + 1))
        return jnp.pad(value, ((0, 0), (0, pad)), constant_values=-1)

    share = jnp.where(
        jnp.arange(SUBLANES * (TEACH + 1)) % (TEACH + 1) == TEACH, 1.0, 1.0 / TEACH
    ).astype(jnp.float32)
    share = jnp.pad(share, (0, pad))[None, :]
    entries = share.shape[1]
    per_step = 8
    return pl.pallas_call(
        functools.partial(frequency_kernel, per_step),
        name="frequencies",
        grid=(groups // per_step,),
        in_specs=[
            pl.BlockSpec((per_step, entries), lambda i: (i, 0)),
            pl.BlockSpec((per_step, entries), lambda i: (i, 0)),
            pl.BlockSpec((1, entries), lambda i: (0, 0)),
        ],
        out_specs=pl.BlockSpec((per_step * SUBLANES, vocab_rows), lambda i: (i, 0)),
        out_shape=jax.ShapeDtypeStruct((positions, vocab_rows), jnp.float32),
        cost_estimate=pl.CostEstimate(
            flops=2 * groups * entries * vocab_rows * SUBLANES,
            bytes_accessed=4 * positions * vocab_rows,
            transcendentals=0,
        ),
    )(packed(high), packed(low), share)


def row_kernel(chunks, chunk, block, offsets, source, target, g_ref, dense_ref, out_ref, sum_ref, held):
    step = pl.program_id(0)

    @pl.when(step == 0)
    def _():
        sum_ref[...] = jnp.zeros_like(sum_ref)

        def clear(i, carry):
            held[pl.ds(i * 8, 8)] = jnp.zeros((8, SUBLANES, LANES), jnp.float32)
            return carry

        lax.fori_loop(0, held.shape[0] // 8, clear, 0)

    @pl.when(step < chunks)
    def _():
        def add(i, carry):
            row = target[i]
            held[row] = held[row] + g_ref[source[i] - step * chunk].astype(jnp.float32)
            return carry

        lax.fori_loop(offsets[step], offsets[step + 1], add, 0)

    @pl.when(step >= chunks)
    def _():
        start = pl.multiple_of((step - chunks) * block, block)
        width = out_ref.shape[1]
        for part in range(-(-width // LANES)):
            low, high = part * LANES, min(width, (part + 1) * LANES)
            total = held[pl.ds(start, block), part, :][:, : high - low] + dense_ref[:, low:high]
            out_ref[:, low:high] = total
            squares = total * total
            folded = jnp.sum(squares.reshape(block // SUBLANES, SUBLANES, high - low), axis=0)
            sum_ref[:, : high - low] += folded


def add_rows(rows, source, target, offsets, dense, chunk):
    vocab_rows, width = dense.shape
    chunks = rows.shape[0] // chunk
    block = 256
    blocks = vocab_rows // block
    return pl.pallas_call(
        functools.partial(row_kernel, chunks, chunk, block),
        name="add_rows",
        grid_spec=pltpu.PrefetchScalarGridSpec(
            num_scalar_prefetch=3,
            grid=(chunks + blocks,),
            in_specs=[
                pl.BlockSpec(
                    (chunk, SUBLANES, LANES), lambda i, *_: (jnp.minimum(i, chunks - 1), 0, 0)
                ),
                pl.BlockSpec((block, width), lambda i, *_: (jnp.maximum(i - chunks, 0), 0)),
            ],
            out_specs=[
                pl.BlockSpec((block, width), lambda i, *_: (jnp.maximum(i - chunks, 0), 0)),
                pl.BlockSpec((SUBLANES, LANES), lambda i, *_: (0, 0)),
            ],
            scratch_shapes=[pltpu.VMEM((vocab_rows, SUBLANES, LANES), jnp.float32)],
        ),
        out_shape=[
            jax.ShapeDtypeStruct((vocab_rows, width), jnp.float32),
            jax.ShapeDtypeStruct((SUBLANES, LANES), jnp.float32),
        ],
        compiler_params=pltpu.CompilerParams(vmem_limit_bytes=48 << 20),
        cost_estimate=pl.CostEstimate(
            flops=rows.shape[0] * 1024,
            bytes_accessed=2 * rows.size + 8 * dense.size,
            transcendentals=0,
        ),
    )(offsets, source, target, rows, dense)


def on_device(
    tokens,
    lengths,
    loss_positions,
    teacher_ids,
    label_ids,
    embedding,
    incoming,
    outgoing,
    expand,
    contract,
    scales,
    drift_embedding,
    incoming_first_moment,
    drift_outgoing,
    drift_expand,
    drift_contract,
    drift_scales,
    power_embedding,
    incoming_second_moment,
    power_outgoing,
    power_expand,
    power_contract,
    power_scales,
):
    ranks = lax.axis_size(PLANE)
    planes = lax.axis_size("fsdp")
    seq_rank = lax.axis_index(PLANE)
    plane = lax.axis_index("fsdp")
    batches, _, slots = tokens.shape
    rows = slots // ranks
    local = batches * rows
    first_row = seq_rank * rows
    vocab_rows, width = embedding.shape
    vocab_start = seq_rank * vocab_rows
    wanted = loss_positions.shape[2]
    own_count = batches * wanted
    count_all = planes * own_count
    query_width = QUERY_HEADS * HEAD_SIZE
    key_width = KEY_VALUE_HEADS * HEAD_SIZE
    number = 0

    table = embedding.astype(jnp.bfloat16)

    token_rows = tokens[:, 0]
    wire_ids = token_rows.reshape(batches, ranks, rows).transpose(1, 0, 2).reshape(-1) - vocab_start
    inside = (wire_ids >= 0) & (wire_ids < vocab_rows)
    found = jnp.take(table, jnp.where(inside, wire_ids, 0), axis=0)
    residual = lax.psum_scatter(
        jnp.where(inside[:, None], found, jnp.zeros((), jnp.bfloat16)),
        PLANE,
        scatter_dimension=0,
        tiled=True,
    ).astype(jnp.float32)

    def whole(master):
        return lax.all_gather(master.astype(jnp.bfloat16), SHARDS, axis=1, tiled=True)

    w_in = whole(incoming)[number]
    gains = whole(scales).astype(jnp.float32)
    w_out = whole(outgoing)[number]
    w_expand = whole(expand)[number]
    w_contract = whole(contract)[number]
    gain_attn, gain_ffn, gain_final = gains[0], gains[1], gains[2]

    teacher_all = lax.all_gather(teacher_ids[:, 0], "fsdp").reshape(count_all, TEACH)
    label_all = lax.all_gather(label_ids[:, 0], "fsdp").reshape(count_all)
    tokens_all = lax.all_gather(token_rows, "fsdp")
    frequencies = frequencies_of(teacher_all, label_all, vocab_start, vocab_rows)

    entry_ids = (
        tokens_all.reshape(planes, batches, ranks, rows).transpose(0, 2, 1, 3).reshape(-1)
        - vocab_start
    )
    entry_count = entry_ids.shape[0]
    entry_inside = (entry_ids >= 0) & (entry_ids < vocab_rows)
    entry_index = jnp.arange(entry_count, dtype=jnp.int32)
    source = lax.sort(jnp.where(entry_inside, entry_index, entry_count)) % entry_count
    target = jnp.clip(jnp.take(entry_ids, source), 0, vocab_rows - 1)
    chunk = 1024
    per_chunk = jnp.sum(entry_inside.reshape(-1, chunk).astype(jnp.int32), axis=1)
    offsets = jnp.concatenate([jnp.zeros((1,), jnp.int32), jnp.cumsum(per_chunk)])

    places = jnp.tile(first_row + jnp.arange(rows, dtype=jnp.int32), batches)
    cosine, sine = rotary_tables(places)
    cosine, sine = cosine[:, None, :], sine[:, None, :]
    bounds = jnp.concatenate([first_row[None].astype(jnp.int32), lengths[:, 0]])
    normed, attn_pull = jax.vjp(rmsnorm, residual, gain_attn)
    normed_low = normed.astype(jnp.bfloat16)
    joined = matmul(normed_low, w_in)
    queries = rotate(
        joined[:, :query_width].reshape(local, QUERY_HEADS, HEAD_SIZE), cosine, sine
    ).astype(jnp.bfloat16)
    keys = rotate(
        joined[:, query_width : query_width + key_width].reshape(
            local, KEY_VALUE_HEADS, HEAD_SIZE
        ),
        cosine,
        sine,
    ).astype(jnp.bfloat16)
    packed = jnp.concatenate(
        [
            keys.reshape(local, key_width),
            joined[:, query_width + key_width :].astype(jnp.bfloat16),
        ],
        axis=1,
    )
    gathered = (
        lax.all_gather(packed, PLANE)
        .reshape(ranks, batches, rows, 2, KEY_VALUE_HEADS, HEAD_SIZE)
        .transpose(3, 1, 4, 0, 2, 5)
        .reshape(2, batches, KEY_VALUE_HEADS, slots, HEAD_SIZE)
    )

    def to_heads(value):
        return (
            value.reshape(batches, rows, KEY_VALUE_HEADS, GROUP, HEAD_SIZE)
            .transpose(0, 2, 3, 1, 4)
            .reshape(batches, KEY_VALUE_HEADS, GROUP * rows, HEAD_SIZE)
        )

    def from_heads(value):
        return (
            value.reshape(batches, KEY_VALUE_HEADS, GROUP, rows, HEAD_SIZE)
            .transpose(0, 3, 1, 2, 4)
            .reshape(local, query_width)
        )

    query_heads = to_heads(queries)
    mixed, log_total_heads = attention_forward(bounds, query_heads, gathered[0], gathered[1])
    attended = from_heads(mixed)
    middle = residual + matmul(attended, w_out)
    normed_ffn, ffn_pull = jax.vjp(rmsnorm, middle, gain_ffn)
    normed_ffn_low = normed_ffn.astype(jnp.bfloat16)
    hidden, act_pull = jax.vjp(
        lambda both: jax.nn.silu(both[:, :FF]) * both[:, FF:], matmul(normed_ffn_low, w_expand)
    )
    hidden_low = hidden.astype(jnp.bfloat16)
    result = middle + matmul(hidden_low, w_contract)

    final, final_pull = jax.vjp(rmsnorm, result, gain_final)
    final_low = final.astype(jnp.bfloat16).reshape(batches, rows, width)
    spots = loss_positions[:, 0] % lengths[:, :1]
    picker = spots[:, :, None] == (first_row + jnp.arange(rows, dtype=jnp.int32))[None, None, :]
    picked = jnp.einsum(
        "bpr,brd->bpd", picker.astype(jnp.bfloat16), final_low, preferred_element_type=jnp.float32
    ).astype(jnp.bfloat16)
    chosen = lax.all_gather(
        lax.psum(picked.reshape(own_count, width), PLANE), "fsdp", axis=0, tiled=True
    )
    logits = against(chosen, table)
    top = jnp.max(logits, axis=1)
    total = jnp.sum(jnp.exp(logits - top[:, None]), axis=1)
    target_part = jnp.sum(frequencies * logits, axis=1)
    stats = lax.all_gather(jnp.stack([top, total, target_part]), PLANE)
    top_all = jnp.max(stats[:, 0], axis=0)
    total_all = jnp.sum(stats[:, 1] * jnp.exp(stats[:, 0] - top_all[None]), axis=0)
    target_all = jnp.sum(stats[:, 2], axis=0)
    log_total = top_all + jnp.log(total_all)
    teacher = teacher_ids[:, 0].reshape(own_count, TEACH)
    counts = jnp.sum((teacher[:, :, None] == teacher[:, None, :]).astype(jnp.float32), axis=-1)
    entropy_part = jnp.mean(jnp.log(counts / TEACH), axis=1)
    own = plane * own_count
    loss_sum = jnp.sum(
        entropy_part + lax.dynamic_slice_in_dim(2.0 * log_total - target_all, own, own_count)
    )
    grad_logits = (
        (2.0 * jnp.exp(logits - log_total[:, None]) - frequencies) / count_all
    ).astype(jnp.bfloat16)
    own_logits = lax.dynamic_slice_in_dim(grad_logits, own, own_count)
    grad_chosen = lax.psum(matmul(own_logits, table), PLANE).reshape(batches, wanted, width)
    grad_final = rounded(
        jnp.einsum(
            "bpr,bpd->brd",
            picker.astype(jnp.float32),
            grad_chosen,
            precision=lax.Precision.HIGHEST,
        ).reshape(local, width)
    )
    grad_residual, grad_gain_final = final_pull(grad_final)
    dense = across(grad_logits, chosen)

    branch = grad_residual.astype(jnp.bfloat16)
    grad_contract = across(hidden_low, branch)
    grad_hidden = rounded(against(branch, w_contract))
    grad_gate_up = act_pull(grad_hidden)[0].astype(jnp.bfloat16)
    grad_expand = across(normed_ffn_low, grad_gate_up)
    grad_normed = rounded(against(grad_gate_up, w_expand))
    grad_middle, grad_gain_ffn = ffn_pull(grad_normed)
    grad_middle = grad_middle + grad_residual
    branch = grad_middle.astype(jnp.bfloat16)
    grad_outgoing = across(attended, branch)
    grad_attended = against(branch, w_out).astype(jnp.bfloat16)
    dq, dk, dv = attention_backward(
        bounds, query_heads, gathered[0], gathered[1], to_heads(grad_attended), log_total_heads
    )
    grad_pair = (
        jnp.stack([dk, dv])
        .reshape(2, batches, KEY_VALUE_HEADS, ranks, rows, HEAD_SIZE)
        .transpose(3, 1, 4, 0, 2, 5)
        .reshape(ranks * local, 2 * key_width)
    )
    grad_pair = lax.psum_scatter(grad_pair, PLANE, scatter_dimension=0, tiled=True)
    grad_queries = rotate(
        from_heads(dq).reshape(local, QUERY_HEADS, HEAD_SIZE), cosine, -sine
    ).reshape(local, query_width)
    grad_keys = rotate(
        grad_pair[:, :key_width].reshape(local, KEY_VALUE_HEADS, HEAD_SIZE), cosine, -sine
    ).reshape(local, key_width)
    grad_joined = jnp.concatenate(
        [grad_queries, grad_keys, grad_pair[:, key_width:]], axis=1
    ).astype(jnp.bfloat16)
    grad_incoming = across(normed_low, grad_joined)
    grad_normed = rounded(against(grad_joined, w_in))
    grad_input, grad_gain_attn = attn_pull(grad_normed)
    grad_rows = (grad_input + grad_middle).astype(jnp.bfloat16)

    tile = SUBLANES * LANES
    padded = jnp.pad(grad_rows, ((0, 0), (0, tile - width))).reshape(local, SUBLANES, LANES)
    rows_all = lax.all_gather(padded, EVERYONE, axis=0, tiled=True)
    table_total, table_squares = add_rows(rows_all, source, target, offsets, dense, chunk)

    def reduced(grad):
        part = lax.psum_scatter(grad, SHARDS, scatter_dimension=1, tiled=True)
        return lax.psum(part, "context")

    layer_totals = (
        reduced(grad_incoming[None]),
        reduced(grad_outgoing[None]),
        reduced(grad_expand[None]),
        reduced(grad_contract[None]),
        reduced(jnp.stack([grad_gain_attn, grad_gain_ffn, grad_gain_final])),
    )
    lead_context = (lax.axis_index("context") == 0).astype(jnp.float32)
    lead_plane = (plane == 0).astype(jnp.float32)
    lead_seq = (seq_rank == 0).astype(jnp.float32)
    layer_square = sum((jnp.sum(grad * grad) for grad in layer_totals))
    sums = lax.psum(
        jnp.stack(
            [
                lead_context * layer_square + lead_plane * jnp.sum(table_squares),
                lead_seq * loss_sum,
            ]
        ),
        EVERYONE,
    )
    grad_norm = jnp.sqrt(sums[0])
    loss_value = sums[1] / count_all
    factor = CLIP / jnp.maximum(grad_norm, CLIP)
    weights = (embedding, incoming, outgoing, expand, contract, scales)
    grads = (table_total,) + layer_totals
    drifts = (
        drift_embedding,
        incoming_first_moment,
        drift_outgoing,
        drift_expand,
        drift_contract,
        drift_scales,
    )
    powers = (
        power_embedding,
        incoming_second_moment,
        power_outgoing,
        power_expand,
        power_contract,
        power_scales,
    )
    rates = (RATE_MATRIX, RATE_MATRIX, RATE_MATRIX, RATE_MATRIX, RATE_MATRIX, RATE_GAIN)
    decays = (DECAY, DECAY, DECAY, DECAY, DECAY, 0.0)
    updated = [
        adamw(
            weights[index],
            grads[index] * factor,
            drifts[index],
            powers[index],
            rates[index],
            decays[index],
        )
        for index in range(6)
    ]
    return (
        (loss_value, grad_norm)
        + tuple(entry[0] for entry in updated)
        + tuple(entry[1] for entry in updated)
        + tuple(entry[2] for entry in updated)
    )


def solution(mesh):
    ids = P(None, "fsdp", None)
    vocab = P(PLANE, None)
    matrix = P(None, SHARDS, None)
    state = (vocab, matrix, matrix, matrix, matrix, P(None, SHARDS))
    in_specs = (ids, P(None, "fsdp"), ids, P(None, "fsdp", None, None), ids) + state * 3
    out_specs = (P(), P()) + state * 3
    return jax.shard_map(
        on_device, mesh=mesh, in_specs=in_specs, out_specs=out_specs, check_vma=False
    )
```
